32 devices in a mesh: rows: 4 (over y, x), cols: 8 (over z, core).
Axes of the slice: x: 2, y: 2, z: 4, core: 2. Of those that a mesh axis runs over, the one named last changes fastest.
Arguments:
- data_tile: bfloat16 [1024, 8192], P('rows', 'cols'), may hold values from 0.05 to 5
- w_factor: float32 [32, 1024], P(None, ('rows', 'cols')), may hold values from 0.05 to 0.5
- h_factor: float32 [32, 8192], P(None, ('cols', 'rows')), may hold values from 0.05 to 0.5
Outputs:
- w_final: float32 [32, 1024], P(None, ('rows', 'cols'))
- h_final: float32 [32, 8192], P(None, ('cols', 'rows'))
The draws below stay inside these ranges and needn't reach their ends.
All inputs are finite; a program needn't handle non-finite values.
Results may differ from the reference program's by a relative error of at most 0.00049.
Values may be sent and summed in bfloat16 or wider, within the bound.
A program may use at most 64 MiB of HBM per device.

```python
import math
import jax
import jax.numpy as jnp
from jax import lax

RANK = 32
TR = 256
TC = 1024
ITERS = 2
M = 1024
N = 8192
N_ROWS = 4


def block_offsets(key, block_count, block_length, spread):
    offsets = jax.random.uniform(key, (block_count,), jnp.float32, -spread, spread)
    return jnp.repeat(offsets, block_length, total_repeat_length=block_count * block_length)


def draw_data_tile(key, part):
    row_key, col_key, cell_key = jax.random.split(key, 3)
    row_part = block_offsets(row_key, M // TR, TR, 1.2)
    col_part = block_offsets(col_key, N // TC, TC, 1.2)
    cell_part = jax.random.uniform(cell_key, (M, N), jnp.float32, -1.5, 1.5)
    log_values = math.log(0.5) + cell_part + row_part[:, None] + col_part[None, :]
    return jnp.exp(jnp.clip(log_values, math.log(0.05), math.log(5.0))).astype(jnp.bfloat16)


def level_of(key, dims, shards, low, top_value):
    gain, own = 1.0, jax.random.fold_in(key, 6)
    for axis_at, blocks in shards:
        draws = jnp.exp(jax.random.uniform(jax.random.fold_in(own, axis_at), (blocks,), jnp.float32, low / len(shards), top_value / len(shards)))
        gain = gain * jnp.repeat(draws, dims[axis_at] // blocks).reshape([-1 if axis == axis_at else 1 for axis in range(len(dims))])
    return gain


def setup_inputs(seed: int = 0) -> dict:
    seeds = jax.random.split(jax.random.key(seed), 4)
    data_tile = draw_data_tile(jax.random.fold_in(seeds[3], 71), 0)
    w_factor = jnp.clip(jnp.exp(math.log(0.5) - 2.3025851 * jax.random.uniform(seeds[1], (RANK, M), jnp.float32) ** level_of(seeds[1], (RANK, M), ((1, 32),), -0.2, 0.2)), 0.05, 0.5)
    h_factor = jnp.clip(jnp.exp(math.log(0.5) - 2.3025851 * jax.random.uniform(seeds[2], (RANK, N), jnp.float32) ** level_of(seeds[2], (RANK, N), ((1, 32),), -0.2, 0.2)), 0.05, 0.5)
    return {"data_tile": data_tile, "w_factor": w_factor, "h_factor": h_factor}


damping = 0.75


def reference(data_tile, w_factor, h_factor):
    blocks = data_tile.reshape(N_ROWS, TR, N)
    w_now = w_factor
    h_now = h_factor
    for rounds in range(ITERS):
        w_round = w_now.astype(jnp.bfloat16)
        h_round = h_now.astype(jnp.bfloat16)
        w_blocks = jnp.moveaxis(w_round.reshape(RANK, N_ROWS, TR), 1, 0)

        def one_block(running, pieces):
            x_block, w_block = pieces
            approx = jnp.dot(w_block.T, h_round, preferred_element_type=jnp.float32)
            quotient = (x_block.astype(jnp.float32) / approx).astype(jnp.bfloat16)
            h_part = jnp.dot(w_block, quotient, preferred_element_type=jnp.float32)
            w_part = jnp.dot(h_round, quotient.T, preferred_element_type=jnp.float32)
            return running + h_part, w_part

        h_numer, w_parts = lax.scan(one_block, jnp.zeros((RANK, N), jnp.float32), (blocks, w_blocks))
        w_numer = jnp.moveaxis(w_parts, 0, 1).reshape(RANK, M)
        w_total = jnp.sum(w_round.astype(jnp.float32), axis=1)
        h_total = jnp.sum(h_round.astype(jnp.float32), axis=1)
        h_next = h_now * ((1.0 - damping) + damping * h_numer / w_total[:, None])
        w_next = w_now * ((1.0 - damping) + damping * w_numer / h_total[:, None])
        w_now = w_next
        h_now = h_next
    return w_now, h_now
```

```python
import functools

import jax
import jax.numpy as jnp
from jax import lax
from jax.experimental import pallas as pl
from jax.experimental.pallas import tpu as pltpu
from jax.sharding import PartitionSpec as P

ITERS = 2

damping = 0.75

MESH = pl.DeviceIdType.MESH
SUB = 8
LANES = 128


def partner(me, d, n):
    if n & (n - 1) == 0:
        out, bit = me, 1
        while bit < n:
            if d & bit:
                out = out + bit * (1 - 2 * (lax.rem(lax.div(me, bit), 2)))
            bit *= 2
        return out
    return lax.rem(d + n - me, n)


def fold(block):
    return jnp.concatenate([block[s : s + SUB] for s in range(0, block.shape[0], SUB)], axis=1)


def unfold(dense, groups, width):
    return jnp.concatenate([dense[:, s * width : (s + 1) * width] for s in range(groups)], axis=0)


def kernel(
    rows, cols, data_hbm, w_hbm, h_hbm, w_out, h_out,
    data_v, w_in, h_own, w_own, w_slots, h_slots, h_send, h_recv, w_send, w_recv,
    local_sem, wg_s, wg_r, hg_s, hg_r, hr_s, hr_r, wr_s, wr_r,
):
    c, r = lax.axis_index("cols"), lax.axis_index("rows")
    rank, wp = w_hbm.shape
    hp = h_hbm.shape[1]
    tr, tc = data_v.shape
    groups = rank // SUB
    used = groups * wp

    load_w = pltpu.make_async_copy(w_hbm, w_in, local_sem.at[0])
    load_h = pltpu.make_async_copy(h_hbm, h_own, local_sem.at[1])
    load_data = pltpu.make_async_copy(data_hbm, data_v, local_sem.at[2])
    load_w.start()
    load_h.start()
    load_data.start()

    c_peers = [(d, partner(c, d, cols)) for d in range(1, cols)]
    r_peers = [(d, partner(r, d, rows)) for d in range(1, rows)]
    barrier = pltpu.get_barrier_semaphore()
    for d, p in c_peers:
        pl.semaphore_signal(barrier, inc=1, device_id={"cols": p}, device_id_type=MESH)
    for d, p in r_peers:
        pl.semaphore_signal(barrier, inc=1, device_id={"rows": p}, device_id_type=MESH)

    load_w.wait()
    load_h.wait()

    def put_w(it, dense):
        w_own[it, :, 0:used] = dense

    put_w(0, fold(w_in[...]))
    h_slots[0, 0] = h_own[...].astype(jnp.bfloat16)
    pl.semaphore_wait(barrier, cols - 1 + rows - 1)

    pending = []

    def send(src, dst, s_sem, r_sem, where):
        copy = pltpu.make_async_remote_copy(
            src_ref=src, dst_ref=dst, send_sem=s_sem, recv_sem=r_sem, device_id=where, device_id_type=MESH
        )
        copy.start()
        pending.append(copy)
        return copy

    def gather_w(it):
        return [
            send(w_own.at[it], w_slots.at[it, c], wg_s.at[it, d], wg_r.at[it, d], {"cols": p})
            for d, p in reversed(c_peers)
        ]

    def gather_h(it):
        return {
            d: send(h_slots.at[it, 0], h_slots.at[it, d], hg_s.at[it, d], hg_r.at[it, d], {"rows": p})
            for d, p in reversed(r_peers)
        }

    w_copies = gather_w(0)
    h_copies = gather_h(0)
    w_dense = w_own[0, :, 0:used]
    h_now = h_own[...]

    for it in range(ITERS):
        w_slots[it, c] = w_own[it]
        for copy in w_copies:
            copy.wait_recv()
        w_f32 = jnp.concatenate(
            [
                jnp.concatenate([w_slots[it, p, :, s * wp : (s + 1) * wp] for p in range(cols)], axis=1)
                for s in range(groups)
            ],
            axis=0,
        )
        w_block = w_f32.astype(jnp.bfloat16)
        w_rows = w_f32.T.astype(jnp.bfloat16)
        w_sum = jnp.sum(w_block.astype(jnp.float32), axis=1, keepdims=True)
        w_sum = fold(jnp.broadcast_to(w_sum, (rank, hp // groups)))
        if it == 0:
            load_data.wait()
        w_part = jnp.zeros((rank, tr), jnp.float32)
        h_sum = jnp.zeros((rank, 1), jnp.float32)
        h_sends = []
        for d in range(rows):
            p = r if d == 0 else r_peers[d - 1][1]
            if d > 0:
                h_copies[d].wait_recv()
            h_piece = h_slots[it, d]
            approx = jnp.dot(w_rows, h_piece, preferred_element_type=jnp.float32)
            if hp % LANES == 0:
                data = data_v[:, pl.ds(pl.multiple_of(p * hp, hp), hp)]
            else:
                per = LANES // hp
                base = pl.multiple_of(lax.div(p, per) * LANES, LANES)
                wide = data_v[:, pl.ds(base, LANES)].astype(jnp.float32)
                data = wide[:, 0:hp]
                for k in range(1, per):
                    data = jnp.where(lax.rem(p, per) == k, wide[:, k * hp : (k + 1) * hp], data)
            quotient = (data.astype(jnp.float32) / approx).astype(jnp.bfloat16)
            h_part = jnp.dot(w_block, quotient, preferred_element_type=jnp.float32)
            h_send[it, d, 0:rank] = h_part
            h_send[it, d, rank : rank + SUB] = w_sum
            if d > 0:
                h_sends.append(
                    send(h_send.at[it, d], h_recv.at[it, d], hr_s.at[it, d], hr_r.at[it, d], {"rows": p})
                )
            w_part += lax.dot_general(
                h_piece, quotient, (((1,), (1,)), ((), ())), preferred_element_type=jnp.float32
            )
            h_sum += jnp.sum(h_piece.astype(jnp.float32), axis=1, keepdims=True)

        h_sum = fold(jnp.broadcast_to(h_sum, (rank, wp)))
        for p in range(cols):
            w_send[it, p, 0, :, 0:used] = fold(w_part[:, p * wp : (p + 1) * wp])
            w_send[it, p, 1, :, 0:used] = h_sum
        w_sends = [
            send(w_send.at[it, p], w_recv.at[it, d], wr_s.at[it, d], wr_r.at[it, d], {"cols": p})
            for d, p in reversed(c_peers)
        ]

        total = h_send[it, 0]
        for copy in h_sends:
            copy.wait_recv()
        for d, p in r_peers:
            total += h_recv[it, d]
        w_total = unfold(total[rank : rank + SUB], groups, hp // groups)[:, 0:1]
        h_now = h_now * (1.0 - damping + damping * total[0:rank] / w_total)
        if it + 1 < ITERS:
            h_slots[it + 1, 0] = h_now.astype(jnp.bfloat16)
            h_copies = gather_h(it + 1)
        else:
            h_out[...] = h_now

        total = w_send[it, c]
        for copy in w_sends:
            copy.wait_recv()
        for d, p in c_peers:
            total += w_recv[it, d]
        numer, h_total = total[0, :, 0:used], total[1, :, 0:used]
        w_dense = w_dense * (1.0 - damping + damping * numer / h_total)
        if it + 1 < ITERS:
            put_w(it + 1, w_dense)
            w_copies = gather_w(it + 1)
        else:
            w_out[...] = unfold(w_dense, groups, wp)

    for copy in pending:
        copy.wait_send()


def solution(mesh):
    rows, cols = mesh.shape["rows"], mesh.shape["cols"]

    def shards(data_tile, w_factor, h_factor):
        rank, wp = w_factor.shape
        hp = h_factor.shape[1]
        wide = pl.cdiv(rank // SUB * wp, LANES) * LANES
        vmem, dma = pltpu.VMEM, pltpu.SemaphoreType.DMA
        return pl.pallas_call(
            functools.partial(kernel, rows, cols),
            out_shape=(
                jax.ShapeDtypeStruct(w_factor.shape, jnp.float32),
                jax.ShapeDtypeStruct(h_factor.shape, jnp.float32),
            ),
            in_specs=[pl.BlockSpec(memory_space=pl.ANY)] * 3,
            out_specs=(pl.BlockSpec(memory_space=pltpu.VMEM),) * 2,
            scratch_shapes=[
                vmem(data_tile.shape, jnp.bfloat16),
                vmem(w_factor.shape, jnp.float32),
                vmem(h_factor.shape, jnp.float32),
                vmem((ITERS, SUB, wide), jnp.float32),
                vmem((ITERS, cols, SUB, wide), jnp.float32),
                vmem((ITERS, rows, rank, hp), jnp.bfloat16),
                vmem((ITERS, rows, rank + SUB, hp), jnp.float32),
                vmem((ITERS, rows, rank + SUB, hp), jnp.float32),
                vmem((ITERS, cols, 2, SUB, wide), jnp.float32),
                vmem((ITERS, cols, 2, SUB, wide), jnp.float32),
                dma((3,)),
                dma((ITERS, cols)),
                dma((ITERS, cols)),
                dma((ITERS, rows)),
                dma((ITERS, rows)),
                dma((ITERS, rows)),
                dma((ITERS, rows)),
                dma((ITERS, cols)),
                dma((ITERS, cols)),
            ],
            compiler_params=pltpu.CompilerParams(collective_id=0, has_side_effects=True),
        )(data_tile, w_factor, h_factor)

    placed = (P("rows", "cols"), P(None, ("rows", "cols")), P(None, ("cols", "rows")))
    return jax.shard_map(
        shards,
        mesh=mesh,
        in_specs=placed,
        out_specs=(P(None, ("rows", "cols")), P(None, ("cols", "rows"))),
        check_vma=False,
    )
```

```python
import functools

import jax
import jax.numpy as jnp
from jax import lax
from jax.experimental import pallas as pl
from jax.experimental.pallas import tpu as pltpu
from jax.sharding import PartitionSpec as P

ITERS = 2

damping = 0.75

MESH = pl.DeviceIdType.MESH
SUB = 8
LANES = 128


def partner(me, d, n):
    if n & (n - 1) == 0:
        out, bit = me, 1
        while bit < n:
            if d & bit:
                out = out + bit * (1 - 2 * (lax.rem(lax.div(me, bit), 2)))
            bit *= 2
        return out
    return lax.rem(d + n - me, n)


def fold(block):
    return jnp.concatenate([block[s : s + SUB] for s in range(0, block.shape[0], SUB)], axis=1)


def unfold(dense, groups, width):
    return jnp.concatenate([dense[:, s * width : (s + 1) * width] for s in range(groups)], axis=0)


def chunk_order(it, rows):
    return [*range(rows - 1, 0, -1), 0]


def as_column(row, rank):
    spread = jnp.broadcast_to(row[:, 0:rank], (rank, rank))
    at = lax.broadcasted_iota(jnp.int32, (rank, rank), 0) == lax.broadcasted_iota(jnp.int32, (rank, rank), 1)
    return jnp.sum(jnp.where(at, spread, 0.0), axis=1, keepdims=True)


def kernel(
    rows, cols, data_hbm, w_hbm, h_hbm, w_out, h_out,
    data_v, w_in, h_own, w_own, w_slots, h_slots, h_send, h_recv, w_send, w_recv,
    pair_send, pair_recv, chip_sums, half_send, half_recv,
    local_sem, wg_s, wg_r, hg_s, hg_r, hr_s, hr_r, wr_s, wr_r, ps_s, ps_r, cs_s, cs_r, hf_s, hf_r,
):
    c, r = lax.axis_index("cols"), lax.axis_index("rows")
    rank, wp = w_hbm.shape
    hp = h_hbm.shape[1]
    tr, tc = data_v.shape
    groups = rank // SUB
    used = groups * wp
    half = tr // 2
    chips = cols // 2
    chip, core = lax.div(c, 2), lax.rem(c, 2)

    load_w = pltpu.make_async_copy(w_hbm, w_in, local_sem.at[0])
    load_h = pltpu.make_async_copy(h_hbm, h_own, local_sem.at[1])
    load_data = pltpu.make_async_copy(data_hbm, data_v, local_sem.at[2])
    load_w.start()
    load_h.start()
    load_data.start()

    c_peers = [(d, partner(c, d, cols)) for d in range(1, cols)]
    r_peers = [(d, partner(r, d, rows)) for d in range(1, rows)]
    chip_peers = [(d, 2 * partner(chip, d, chips) + core) for d in range(1, chips)]
    barrier = pltpu.get_barrier_semaphore()
    for d, p in reversed(c_peers):
        pl.semaphore_signal(barrier, inc=1, device_id={"cols": p}, device_id_type=MESH)
    for d, p in reversed(r_peers):
        pl.semaphore_signal(barrier, inc=1, device_id={"rows": p}, device_id_type=MESH)

    load_w.wait()
    load_h.wait()
    w_own[:, 0:used] = fold(w_in[...])
    h_slots[0, 0] = h_own[...].astype(jnp.bfloat16)
    pl.semaphore_wait(barrier, cols - 1 + rows - 1)

    pending = []

    def send(src, dst, s_sem, r_sem, where):
        copy = pltpu.make_async_remote_copy(
            src_ref=src, dst_ref=dst, send_sem=s_sem, recv_sem=r_sem, device_id=where, device_id_type=MESH
        )
        copy.start()
        pending.append(copy)
        return copy

    def gather_h(it):
        return {
            d: send(h_slots.at[it, 0], h_slots.at[it, d], hg_s.at[it, d], hg_r.at[it, d], {"rows": p})
            for d, p in reversed(r_peers)
        }

    w_copies = [
        send(w_own, w_slots.at[c], wg_s.at[d], wg_r.at[d], {"cols": p}) for d, p in reversed(c_peers)
    ]
    h_copies = gather_h(0)
    h_now = h_own[...]
    w_slots[c] = w_own[...]
    load_data.wait()
    for copy in w_copies:
        copy.wait_recv()
    w_f32 = jnp.concatenate(
        [
            jnp.concatenate([w_slots[p, :, s * wp : (s + 1) * wp] for p in range(cols)], axis=1)
            for s in range(groups)
        ],
        axis=0,
    )

    for it in range(ITERS):
        last = it + 1 == ITERS
        w_block = w_f32.astype(jnp.bfloat16)
        w_rows = w_f32.T.astype(jnp.bfloat16)
        w_sum = jnp.sum(w_rows.astype(jnp.float32), axis=0, keepdims=True)
        w_part = jnp.zeros((rank, tr), jnp.float32)
        h_sum = jnp.zeros((SUB, rank), jnp.float32)
        h_sends = []
        for d in chunk_order(it, rows):
            p = r if d == 0 else r_peers[d - 1][1]
            if d > 0:
                h_copies[d].wait_recv()
            h_piece = h_slots[it, d]
            approx = jnp.dot(w_rows, h_piece, preferred_element_type=jnp.float32)
            if hp % LANES == 0:
                data = data_v[:, pl.ds(pl.multiple_of(p * hp, hp), hp)]
            else:
                per = LANES // hp
                base = pl.multiple_of(lax.div(p, per) * LANES, LANES)
                wide = data_v[:, pl.ds(base, LANES)].astype(jnp.float32)
                data = wide[:, 0:hp]
                for k in range(1, per):
                    data = jnp.where(lax.rem(p, per) == k, wide[:, k * hp : (k + 1) * hp], data)
            quotient = (data.astype(jnp.float32) / approx).astype(jnp.bfloat16)
            h_part = jnp.dot(w_block, quotient, preferred_element_type=jnp.float32)
            h_send[it, d, 0:rank] = h_part
            h_send[it, d, rank : rank + 1, 0:rank] = w_sum
            if d > 0:
                h_sends.append(
                    send(h_send.at[it, d], h_recv.at[it, d], hr_s.at[it, d], hr_r.at[it, d], {"rows": p})
                )
            w_part += lax.dot_general(
                h_piece, quotient, (((1,), (1,)), ((), ())), preferred_element_type=jnp.float32
            )
            h_sum += lax.dot_general(
                jnp.ones((SUB, hp), jnp.bfloat16), h_piece, (((1,), (1,)), ((), ())),
                preferred_element_type=jnp.float32,
            )

        if last:
            for p in range(cols):
                w_send[p, 0:SUB, 0:used] = fold(w_part[:, p * wp : (p + 1) * wp])
                w_send[p, SUB : SUB + 1, 0:rank] = h_sum[0:1]
            w_sends = [
                send(w_send.at[p], w_recv.at[d], wr_s.at[d], wr_r.at[d], {"cols": p})
                for d, p in reversed(c_peers)
            ]
        else:
            low, high = w_part[:, 0:half], w_part[:, half:tr]
            pair_send[it, 0:rank] = jnp.where(core == 0, high, low)
            pair_send[it, rank : rank + 1, 0:rank] = h_sum[0:1]
            pair = send(
                pair_send.at[it], pair_recv.at[it], ps_s.at[it], ps_r.at[it], {"cols": c + 1 - 2 * core}
            )
            kept = jnp.where(core == 0, low, high)
            pair.wait_recv()
            chip_sums[it, chip, 0:rank] = kept + pair_recv[it, 0:rank]
            chip_sums[it, chip, rank : rank + 1, 0:rank] = h_sum[0:1] + pair_recv[it, rank : rank + 1, 0:rank]
            chip_sends = [
                send(
                    chip_sums.at[it, chip], chip_sums.at[it, chip], cs_s.at[it, d], cs_r.at[it, d], {"cols": p}
                )
                for d, p in reversed(chip_peers)
            ]

        for copy in h_sends:
            copy.wait_recv()
        numer, total = h_send[it, 0, 0:rank], h_send[it, 0, rank : rank + 1, 0:rank]
        for d, p in r_peers:
            numer += h_recv[it, d, 0:rank]
            total += h_recv[it, d, rank : rank + 1, 0:rank]
        h_now = h_now * (1.0 - damping + damping * numer / as_column(total, rank))
        if last:
            h_out[...] = h_now
        else:
            h_slots[it + 1, 0] = h_now.astype(jnp.bfloat16)
            h_copies = gather_h(it + 1)

        if last:
            w_now = w_f32[:, 0:wp]
            for p in range(1, cols):
                w_now = jnp.where(c == p, w_f32[:, p * wp : (p + 1) * wp], w_now)
            for copy in w_sends:
                copy.wait_recv()
            numer, total = w_send[c, 0:SUB, 0:used], w_send[c, SUB : SUB + 1, 0:rank]
            for d, p in c_peers:
                numer += w_recv[d, 0:SUB, 0:used]
                total += w_recv[d, SUB : SUB + 1, 0:rank]
            numer = unfold(numer, groups, wp)
            w_out[...] = w_now * (1.0 - damping + damping * numer / as_column(total, rank))
        else:
            w_half = jnp.where(core == 0, w_f32[:, 0:half], w_f32[:, half:tr])
            for copy in chip_sends:
                copy.wait_recv()
            numer, total = chip_sums[it, 0, 0:rank], chip_sums[it, 0, rank : rank + 1, 0:rank]
            for p in range(1, chips):
                numer += chip_sums[it, p, 0:rank]
                total += chip_sums[it, p, rank : rank + 1, 0:rank]
            w_half = w_half * (1.0 - damping + damping * numer / as_column(total, rank))
            half_send[it] = w_half
            swap = send(
                half_send.at[it], half_recv.at[it], hf_s.at[it], hf_r.at[it], {"cols": c + 1 - 2 * core}
            )
            swap.wait_recv()
            theirs = half_recv[it]
            w_f32 = jnp.concatenate(
                [jnp.where(core == 0, w_half, theirs), jnp.where(core == 0, theirs, w_half)], axis=1
            )

    for copy in pending:
        copy.wait_send()


def solution(mesh):
    rows, cols = mesh.shape["rows"], mesh.shape["cols"]

    def shards(data_tile, w_factor, h_factor):
        rank, wp = w_factor.shape
        hp = h_factor.shape[1]
        half = data_tile.shape[0] // 2
        wide = pl.cdiv(rank // SUB * wp, LANES) * LANES
        vmem, dma = pltpu.VMEM, pltpu.SemaphoreType.DMA
        return pl.pallas_call(
            functools.partial(kernel, rows, cols),
            out_shape=(
                pltpu.VMEM(w_factor.shape, jnp.float32),
                pltpu.VMEM(h_factor.shape, jnp.float32),
            ),
            in_specs=[pl.BlockSpec(memory_space=pl.ANY)] * 3,
            out_specs=(pl.BlockSpec(memory_space=pltpu.VMEM),) * 2,
            scratch_shapes=[
                vmem(data_tile.shape, jnp.bfloat16),
                vmem(w_factor.shape, jnp.float32),
                vmem(h_factor.shape, jnp.float32),
                vmem((SUB, wide), jnp.float32),
                vmem((cols, SUB, wide), jnp.float32),
                vmem((ITERS, rows, rank, hp), jnp.bfloat16),
                vmem((ITERS, rows, rank + 1, hp), jnp.float32),
                vmem((ITERS, rows, rank + 1, hp), jnp.float32),
                vmem((cols, SUB + 1, wide), jnp.float32),
                vmem((cols, SUB + 1, wide), jnp.float32),
                vmem((ITERS, rank + 1, half), jnp.float32),
                vmem((ITERS, rank + 1, half), jnp.float32),
                vmem((ITERS, cols // 2, rank + 1, half), jnp.float32),
                vmem((ITERS, rank, half), jnp.float32),
                vmem((ITERS, rank, half), jnp.float32),
                dma((3,)),
                dma((cols,)),
                dma((cols,)),
                dma((ITERS, rows)),
                dma((ITERS, rows)),
                dma((ITERS, rows)),
                dma((ITERS, rows)),
                dma((cols,)),
                dma((cols,)),
                dma((ITERS,)),
                dma((ITERS,)),
                dma((ITERS, cols // 2)),
                dma((ITERS, cols // 2)),
                dma((ITERS,)),
                dma((ITERS,)),
            ],
            compiler_params=pltpu.CompilerParams(collective_id=0, has_side_effects=True),
        )(data_tile, w_factor, h_factor)

    placed = (P("rows", "cols"), P(None, ("rows", "cols")), P(None, ("cols", "rows")))
    return jax.shard_map(
        shards,
        mesh=mesh,
        in_specs=placed,
        out_specs=(P(None, ("rows", "cols")), P(None, ("cols", "rows"))),
        check_vma=False,
    )
```

```python
import functools

import jax
import jax.numpy as jnp
from jax import lax
from jax.experimental import pallas as pl
from jax.experimental.pallas import tpu as pltpu
from jax.sharding import PartitionSpec as P

ITERS = 2

damping = 0.75

MESH = pl.DeviceIdType.MESH
SUB = 8
LANES = 128


def partner(me, d, n):
    if n & (n - 1) == 0:
        out, bit = me, 1
        while bit < n:
            if d & bit:
                out = out + bit * (1 - 2 * (lax.rem(lax.div(me, bit), 2)))
            bit *= 2
        return out
    return lax.rem(d + n - me, n)


def fold(block):
    return jnp.concatenate([block[s : s + SUB] for s in range(0, block.shape[0], SUB)], axis=1)


def unfold(dense, groups, width):
    return jnp.concatenate([dense[:, s * width : (s + 1) * width] for s in range(groups)], axis=0)


def chunk_order(it, rows):
    return [*range(rows - 1, 0, -1), 0]


def as_column(row, rank):
    spread = jnp.broadcast_to(row[:, 0:rank], (rank, rank))
    at = lax.broadcasted_iota(jnp.int32, (rank, rank), 0) == lax.broadcasted_iota(jnp.int32, (rank, rank), 1)
    return jnp.sum(jnp.where(at, spread, 0.0), axis=1, keepdims=True)


def kernel(
    rows, cols, data_hbm, w_hbm, h_hbm, w_out, h_out,
    data_v, w_in, h_own, w_own, w_slots, h_slots, h_send, h_recv, w_send, w_recv,
    pair_send, pair_recv, chip_sums, half_send, half_recv,
    local_sem, wg_s, wg_r, hg_s, hg_r, hr_s, hr_r, wr_s, wr_r, ps_s, ps_r, cs_s, cs_r, hf_s, hf_r,
):
    c, r = lax.axis_index("cols"), lax.axis_index("rows")
    rank, wp = w_hbm.shape
    hp = h_hbm.shape[1]
    tr, tc = data_v.shape
    groups = rank // SUB
    used = groups * wp
    half = tr // 2
    chips = cols // 2
    chip, core = lax.div(c, 2), lax.rem(c, 2)

    load_w = pltpu.make_async_copy(w_hbm, w_in, local_sem.at[0])
    load_h = pltpu.make_async_copy(h_hbm, h_own, local_sem.at[1])
    load_data = pltpu.make_async_copy(data_hbm, data_v, local_sem.at[2])
    load_w.start()
    load_h.start()
    load_data.start()

    c_peers = [(d, partner(c, d, cols)) for d in range(1, cols)]
    r_peers = [(d, partner(r, d, rows)) for d in range(1, rows)]
    chip_peers = [(d, 2 * partner(chip, d, chips) + core) for d in range(1, chips)]
    barrier = pltpu.get_barrier_semaphore()
    for d, p in reversed(c_peers):
        pl.semaphore_signal(barrier, inc=1, device_id={"cols": p}, device_id_type=MESH)
    for d, p in reversed(r_peers):
        pl.semaphore_signal(barrier, inc=1, device_id={"rows": p}, device_id_type=MESH)

    load_w.wait()
    load_h.wait()
    w_own[:, 0:used] = fold(w_in[...])
    h_slots[0, 0] = h_own[...].astype(jnp.bfloat16)
    pl.semaphore_wait(barrier, cols - 1 + rows - 1)

    pending = []

    def send(src, dst, s_sem, r_sem, where):
        copy = pltpu.make_async_remote_copy(
            src_ref=src, dst_ref=dst, send_sem=s_sem, recv_sem=r_sem, device_id=where, device_id_type=MESH
        )
        copy.start()
        pending.append(copy)
        return copy

    def gather_h(it):
        return {
            d: send(h_slots.at[it, 0], h_slots.at[it, d], hg_s.at[it, d], hg_r.at[it, d], {"rows": p})
            for d, p in reversed(r_peers)
        }

    w_copies = [
        send(w_own, w_slots.at[c], wg_s.at[d], wg_r.at[d], {"cols": p}) for d, p in reversed(c_peers)
    ]
    h_copies = gather_h(0)
    h_now = h_own[...]
    w_slots[c] = w_own[...]
    load_data.wait()
    for copy in w_copies:
        copy.wait_recv()
    w_f32 = jnp.concatenate(
        [
            jnp.concatenate([w_slots[p, :, s * wp : (s + 1) * wp] for p in range(cols)], axis=1)
            for s in range(groups)
        ],
        axis=0,
    )

    for it in range(ITERS):
        last = it + 1 == ITERS
        w_block = w_f32.astype(jnp.bfloat16)
        w_rows = w_f32.T.astype(jnp.bfloat16)
        w_sum = jnp.sum(w_rows.astype(jnp.float32), axis=0, keepdims=True)
        w_part = jnp.zeros((rank, tr), jnp.float32)
        h_sum = jnp.zeros((SUB, rank), jnp.float32)
        h_sends = []
        for d in range(1, rows):
            h_copies[d].wait_recv()
        kept_chunks = []
        for d in chunk_order(it, rows):
            p = r if d == 0 else r_peers[d - 1][1]
            h_piece = h_slots[it, d]
            approx = jnp.dot(w_rows, h_piece, preferred_element_type=jnp.float32)
            if hp % LANES == 0:
                data = data_v[:, pl.ds(pl.multiple_of(p * hp, hp), hp)]
            else:
                per = LANES // hp
                base = pl.multiple_of(lax.div(p, per) * LANES, LANES)
                wide = data_v[:, pl.ds(base, LANES)].astype(jnp.float32)
                data = wide[:, 0:hp]
                for k in range(1, per):
                    data = jnp.where(lax.rem(p, per) == k, wide[:, k * hp : (k + 1) * hp], data)
            quotient = (data.astype(jnp.float32) / approx).astype(jnp.bfloat16)
            kept_chunks.append((d, p, h_piece, quotient))
        for d, p, h_piece, quotient in kept_chunks:
            h_part = jnp.dot(w_block, quotient, preferred_element_type=jnp.float32)
            h_send[it, d, 0:rank] = h_part
            h_send[it, d, rank : rank + 1, 0:rank] = w_sum
            if d > 0:
                h_sends.append(
                    send(h_send.at[it, d], h_recv.at[it, d], hr_s.at[it, d], hr_r.at[it, d], {"rows": p})
                )

        for d, p, h_piece, quotient in kept_chunks:
            w_part += lax.dot_general(
                h_piece, quotient, (((1,), (1,)), ((), ())), preferred_element_type=jnp.float32
            )
            h_sum += lax.dot_general(
                jnp.ones((SUB, hp), jnp.bfloat16), h_piece, (((1,), (1,)), ((), ())),
                preferred_element_type=jnp.float32,
            )

        if last:
            for p in range(cols):
                w_send[p, 0:SUB, 0:used] = fold(w_part[:, p * wp : (p + 1) * wp])
                w_send[p, SUB : SUB + 1, 0:rank] = h_sum[0:1]
            w_sends = [
                send(w_send.at[p], w_recv.at[d], wr_s.at[d], wr_r.at[d], {"cols": p})
                for d, p in reversed(c_peers)
            ]
        else:
            low, high = w_part[:, 0:half], w_part[:, half:tr]
            pair_send[it, 0:rank] = jnp.where(core == 0, high, low)
            pair_send[it, rank : rank + 1, 0:rank] = h_sum[0:1]
            pair = send(
                pair_send.at[it], pair_recv.at[it], ps_s.at[it], ps_r.at[it], {"cols": c + 1 - 2 * core}
            )
            kept = jnp.where(core == 0, low, high)
            pair.wait_recv()
            chip_sums[it, chip, 0:rank] = kept + pair_recv[it, 0:rank]
            chip_sums[it, chip, rank : rank + 1, 0:rank] = h_sum[0:1] + pair_recv[it, rank : rank + 1, 0:rank]
            chip_sends = [
                send(
                    chip_sums.at[it, chip], chip_sums.at[it, chip], cs_s.at[it, d], cs_r.at[it, d], {"cols": p}
                )
                for d, p in reversed(chip_peers)
            ]

        for copy in h_sends:
            copy.wait_recv()
        numer, total = h_send[it, 0, 0:rank], h_send[it, 0, rank : rank + 1, 0:rank]
        for d, p in r_peers:
            numer += h_recv[it, d, 0:rank]
            total += h_recv[it, d, rank : rank + 1, 0:rank]
        h_now = h_now * (1.0 - damping + damping * numer / as_column(total, rank))
        if last:
            h_out[...] = h_now
        else:
            h_slots[it + 1, 0] = h_now.astype(jnp.bfloat16)
            h_copies = gather_h(it + 1)

        if last:
            w_now = w_f32[:, 0:wp]
            for p in range(1, cols):
                w_now = jnp.where(c == p, w_f32[:, p * wp : (p + 1) * wp], w_now)
            for copy in w_sends:
                copy.wait_recv()
            numer, total = w_send[c, 0:SUB, 0:used], w_send[c, SUB : SUB + 1, 0:rank]
            for d, p in c_peers:
                numer += w_recv[d, 0:SUB, 0:used]
                total += w_recv[d, SUB : SUB + 1, 0:rank]
            numer = unfold(numer, groups, wp)
            w_out[...] = w_now * (1.0 - damping + damping * numer / as_column(total, rank))
        else:
            w_half = jnp.where(core == 0, w_f32[:, 0:half], w_f32[:, half:tr])
            for copy in chip_sends:
                copy.wait_recv()
            numer, total = chip_sums[it, 0, 0:rank], chip_sums[it, 0, rank : rank + 1, 0:rank]
            for p in range(1, chips):
                numer += chip_sums[it, p, 0:rank]
                total += chip_sums[it, p, rank : rank + 1, 0:rank]
            w_half = w_half * (1.0 - damping + damping * numer / as_column(total, rank))
            half_send[it] = w_half
            swap = send(
                half_send.at[it], half_recv.at[it], hf_s.at[it], hf_r.at[it], {"cols": c + 1 - 2 * core}
            )
            swap.wait_recv()
            theirs = half_recv[it]
            w_f32 = jnp.concatenate(
                [jnp.where(core == 0, w_half, theirs), jnp.where(core == 0, theirs, w_half)], axis=1
            )

    for copy in pending:
        copy.wait_send()


def solution(mesh):
    rows, cols = mesh.shape["rows"], mesh.shape["cols"]

    def shards(data_tile, w_factor, h_factor):
        rank, wp = w_factor.shape
        hp = h_factor.shape[1]
        half = data_tile.shape[0] // 2
        wide = pl.cdiv(rank // SUB * wp, LANES) * LANES
        vmem, dma = pltpu.VMEM, pltpu.SemaphoreType.DMA
        return pl.pallas_call(
            functools.partial(kernel, rows, cols),
            out_shape=(
                pltpu.VMEM(w_factor.shape, jnp.float32),
                pltpu.VMEM(h_factor.shape, jnp.float32),
            ),
            in_specs=[pl.BlockSpec(memory_space=pl.ANY)] * 3,
            out_specs=(pl.BlockSpec(memory_space=pltpu.VMEM),) * 2,
            scratch_shapes=[
                vmem(data_tile.shape, jnp.bfloat16),
                vmem(w_factor.shape, jnp.float32),
                vmem(h_factor.shape, jnp.float32),
                vmem((SUB, wide), jnp.float32),
                vmem((cols, SUB, wide), jnp.float32),
                vmem((ITERS, rows, rank, hp), jnp.bfloat16),
                vmem((ITERS, rows, rank + 1, hp), jnp.float32),
                vmem((ITERS, rows, rank + 1, hp), jnp.float32),
                vmem((cols, SUB + 1, wide), jnp.float32),
                vmem((cols, SUB + 1, wide), jnp.float32),
                vmem((ITERS, rank + 1, half), jnp.float32),
                vmem((ITERS, rank + 1, half), jnp.float32),
                vmem((ITERS, cols // 2, rank + 1, half), jnp.float32),
                vmem((ITERS, rank, half), jnp.float32),
                vmem((ITERS, rank, half), jnp.float32),
                dma((3,)),
                dma((cols,)),
                dma((cols,)),
                dma((ITERS, rows)),
                dma((ITERS, rows)),
                dma((ITERS, rows)),
                dma((ITERS, rows)),
                dma((cols,)),
                dma((cols,)),
                dma((ITERS,)),
                dma((ITERS,)),
                dma((ITERS, cols // 2)),
                dma((ITERS, cols // 2)),
                dma((ITERS,)),
                dma((ITERS,)),
            ],
            compiler_params=pltpu.CompilerParams(collective_id=0, has_side_effects=True),
        )(data_tile, w_factor, h_factor)

    placed = (P("rows", "cols"), P(None, ("rows", "cols")), P(None, ("cols", "rows")))
    return jax.shard_map(
        shards,
        mesh=mesh,
        in_specs=placed,
        out_specs=(P(None, ("rows", "cols")), P(None, ("cols", "rows"))),
        check_vma=False,
    )
```

```python
import functools

import jax
import jax.numpy as jnp
from jax import lax
from jax.experimental import pallas as pl
from jax.experimental.pallas import tpu as pltpu
from jax.sharding import PartitionSpec as P

ITERS = 2

damping = 0.75

MESH = pl.DeviceIdType.MESH
SUB = 8
LANES = 128


def partner(me, d, n):
    if n & (n - 1) == 0:
        out, bit = me, 1
        while bit < n:
            if d & bit:
                out = out + bit * (1 - 2 * (lax.rem(lax.div(me, bit), 2)))
            bit *= 2
        return out
    return lax.rem(d + n - me, n)


def fold(block):
    return jnp.concatenate([block[s : s + SUB] for s in range(0, block.shape[0], SUB)], axis=1)


def unfold(dense, groups, width):
    return jnp.concatenate([dense[:, s * width : (s + 1) * width] for s in range(groups)], axis=0)


def chunk_order(it, rows):
    return [*range(rows - 1, 0, -1), 0]


def as_column(row, rank):
    spread = jnp.broadcast_to(row[:, 0:rank], (rank, rank))
    at = lax.broadcasted_iota(jnp.int32, (rank, rank), 0) == lax.broadcasted_iota(jnp.int32, (rank, rank), 1)
    return jnp.sum(jnp.where(at, spread, 0.0), axis=1, keepdims=True)


def kernel(
    rows, cols, data_hbm, w_hbm, h_hbm, w_out, h_out,
    data_v, w_in, h_own, w_own, w_slots, h_slots, h_send, h_recv, w_send, w_recv,
    pair_send, pair_recv, chip_sums, half_send, half_recv,
    local_sem, wg_s, wg_r, hg_s, hg_r, hr_s, hr_r, wr_s, wr_r, ps_s, ps_r, cs_s, cs_r, hf_s, hf_r,
):
    c, r = lax.axis_index("cols"), lax.axis_index("rows")
    rank, wp = w_hbm.shape
    hp = h_hbm.shape[1]
    tr, tc = data_v.shape
    groups = rank // SUB
    used = groups * wp
    half = tr // 2
    chips = cols // 2
    chip, core = lax.div(c, 2), lax.rem(c, 2)

    load_w = pltpu.make_async_copy(w_hbm, w_in, local_sem.at[0])
    load_h = pltpu.make_async_copy(h_hbm, h_own, local_sem.at[1])
    load_data = pltpu.make_async_copy(data_hbm, data_v, local_sem.at[2])

    c_peers = [(d, partner(c, d, cols)) for d in range(1, cols)]
    r_peers = [(d, partner(r, d, rows)) for d in range(1, rows)]
    chip_peers = [(d, 2 * partner(chip, d, chips) + core) for d in range(1, chips)]
    barrier = pltpu.get_barrier_semaphore()
    for d, p in reversed(c_peers):
        pl.semaphore_signal(barrier, inc=1, device_id={"cols": p}, device_id_type=MESH)
    for d, p in reversed(r_peers):
        pl.semaphore_signal(barrier, inc=1, device_id={"rows": p}, device_id_type=MESH)

    load_w.start()
    load_h.start()
    load_data.start()
    load_w.wait()
    load_h.wait()
    w_own[:, 0:used] = fold(w_in[...])
    h_slots[0, 0] = h_own[...].astype(jnp.bfloat16)
    pl.semaphore_wait(barrier, cols - 1 + rows - 1)

    pending = []

    def send(src, dst, s_sem, r_sem, where):
        copy = pltpu.make_async_remote_copy(
            src_ref=src, dst_ref=dst, send_sem=s_sem, recv_sem=r_sem, device_id=where, device_id_type=MESH
        )
        copy.start()
        pending.append(copy)
        return copy

    def gather_h(it):
        return {
            d: send(h_slots.at[it, 0], h_slots.at[it, d], hg_s.at[it, d], hg_r.at[it, d], {"rows": p})
            for d, p in reversed(r_peers)
        }

    w_copies = [
        send(w_own, w_slots.at[c], wg_s.at[d], wg_r.at[d], {"cols": p}) for d, p in reversed(c_peers)
    ]
    h_copies = gather_h(0)
    h_now = h_own[...]
    w_slots[c] = w_own[...]
    load_data.wait()
    for copy in w_copies:
        copy.wait_recv()
    w_f32 = jnp.concatenate(
        [
            jnp.concatenate([w_slots[p, :, s * wp : (s + 1) * wp] for p in range(cols)], axis=1)
            for s in range(groups)
        ],
        axis=0,
    )

    for it in range(ITERS):
        last = it + 1 == ITERS
        w_block = w_f32.astype(jnp.bfloat16)
        w_rows = w_f32.T.astype(jnp.bfloat16)
        w_sum = jnp.sum(w_rows.astype(jnp.float32), axis=0, keepdims=True)
        w_part = jnp.zeros((rank, tr), jnp.float32)
        h_sum = jnp.zeros((SUB, rank), jnp.float32)
        h_sends = []
        for d in range(1, rows):
            h_copies[d].wait_recv()
        kept_chunks = []
        for d in chunk_order(it, rows):
            p = r if d == 0 else r_peers[d - 1][1]
            h_piece = h_slots[it, d]
            approx = jnp.dot(w_rows, h_piece, preferred_element_type=jnp.float32)
            if hp % LANES == 0:
                data = data_v[:, pl.ds(pl.multiple_of(p * hp, hp), hp)]
            else:
                per = LANES // hp
                base = pl.multiple_of(lax.div(p, per) * LANES, LANES)
                wide = data_v[:, pl.ds(base, LANES)].astype(jnp.float32)
                data = wide[:, 0:hp]
                for k in range(1, per):
                    data = jnp.where(lax.rem(p, per) == k, wide[:, k * hp : (k + 1) * hp], data)
            quotient = (data.astype(jnp.float32) / approx).astype(jnp.bfloat16)
            kept_chunks.append((d, p, h_piece, quotient))
        for d, p, h_piece, quotient in kept_chunks:
            h_part = jnp.dot(w_block, quotient, preferred_element_type=jnp.float32)
            h_send[it, d, 0:rank] = h_part
            h_send[it, d, rank : rank + 1, 0:rank] = w_sum
            if d > 0:
                h_sends.append(
                    send(h_send.at[it, d], h_recv.at[it, d], hr_s.at[it, d], hr_r.at[it, d], {"rows": p})
                )

        for d, p, h_piece, quotient in kept_chunks:
            w_part += lax.dot_general(
                h_piece, quotient, (((1,), (1,)), ((), ())), preferred_element_type=jnp.float32
            )
            h_sum += lax.dot_general(
                jnp.ones((SUB, hp), jnp.bfloat16), h_piece, (((1,), (1,)), ((), ())),
                preferred_element_type=jnp.float32,
            )

        if last:
            for p in range(cols):
                w_send[p, 0:SUB, 0:used] = fold(w_part[:, p * wp : (p + 1) * wp])
                w_send[p, SUB : SUB + 1, 0:rank] = h_sum[0:1]
            w_sends = [
                send(w_send.at[p], w_recv.at[d], wr_s.at[d], wr_r.at[d], {"cols": p})
                for d, p in reversed(c_peers)
            ]
        else:
            low, high = w_part[:, 0:half], w_part[:, half:tr]
            pair_send[it, 0:rank] = jnp.where(core == 0, high, low)
            pair_send[it, rank : rank + 1, 0:rank] = h_sum[0:1]
            pair = send(
                pair_send.at[it], pair_recv.at[it], ps_s.at[it], ps_r.at[it], {"cols": c + 1 - 2 * core}
            )
            kept = jnp.where(core == 0, low, high)
            pair.wait_recv()
            chip_sums[it, chip, 0:rank] = kept + pair_recv[it, 0:rank]
            chip_sums[it, chip, rank : rank + 1, 0:rank] = h_sum[0:1] + pair_recv[it, rank : rank + 1, 0:rank]
            chip_sends = [
                send(
                    chip_sums.at[it, chip], chip_sums.at[it, chip], cs_s.at[it, d], cs_r.at[it, d], {"cols": p}
                )
                for d, p in reversed(chip_peers)
            ]

        for copy in h_sends:
            copy.wait_recv()
        numer, total = h_send[it, 0, 0:rank], h_send[it, 0, rank : rank + 1, 0:rank]
        for d, p in r_peers:
            numer += h_recv[it, d, 0:rank]
            total += h_recv[it, d, rank : rank + 1, 0:rank]
        h_now = h_now * (1.0 - damping + damping * numer / as_column(total, rank))
        if last:
            h_out[...] = h_now
        else:
            h_slots[it + 1, 0] = h_now.astype(jnp.bfloat16)
            h_copies = gather_h(it + 1)

        if last:
            w_now = w_f32[:, 0:wp]
            for p in range(1, cols):
                w_now = jnp.where(c == p, w_f32[:, p * wp : (p + 1) * wp], w_now)
            for copy in w_sends:
                copy.wait_recv()
            numer, total = w_send[c, 0:SUB, 0:used], w_send[c, SUB : SUB + 1, 0:rank]
            for d, p in c_peers:
                numer += w_recv[d, 0:SUB, 0:used]
                total += w_recv[d, SUB : SUB + 1, 0:rank]
            numer = unfold(numer, groups, wp)
            w_out[...] = w_now * (1.0 - damping + damping * numer / as_column(total, rank))
        else:
            w_half = jnp.where(core == 0, w_f32[:, 0:half], w_f32[:, half:tr])
            for copy in chip_sends:
                copy.wait_recv()
            numer, total = chip_sums[it, 0, 0:rank], chip_sums[it, 0, rank : rank + 1, 0:rank]
            for p in range(1, chips):
                numer += chip_sums[it, p, 0:rank]
                total += chip_sums[it, p, rank : rank + 1, 0:rank]
            w_half = w_half * (1.0 - damping + damping * numer / as_column(total, rank))
            half_send[it] = w_half
            swap = send(
                half_send.at[it], half_recv.at[it], hf_s.at[it], hf_r.at[it], {"cols": c + 1 - 2 * core}
            )
            swap.wait_recv()
            theirs = half_recv[it]
            w_f32 = jnp.concatenate(
                [jnp.where(core == 0, w_half, theirs), jnp.where(core == 0, theirs, w_half)], axis=1
            )

    for copy in pending:
        copy.wait_send()


def finish(w_ref, h_ref, w_out, h_out, sems):
    copies = [
        pltpu.make_async_copy(w_ref, w_out, sems.at[0]),
        pltpu.make_async_copy(h_ref, h_out, sems.at[1]),
    ]
    for copy in copies:
        copy.start()
    for copy in copies:
        copy.wait()


def solution(mesh):
    rows, cols = mesh.shape["rows"], mesh.shape["cols"]

    def shards(data_tile, w_factor, h_factor):
        rank, wp = w_factor.shape
        hp = h_factor.shape[1]
        half = data_tile.shape[0] // 2
        wide = pl.cdiv(rank // SUB * wp, LANES) * LANES
        vmem, dma = pltpu.VMEM, pltpu.SemaphoreType.DMA
        w_new, h_new = pl.pallas_call(
            functools.partial(kernel, rows, cols),
            out_shape=(
                pltpu.VMEM(w_factor.shape, jnp.float32),
                pltpu.VMEM(h_factor.shape, jnp.float32),
            ),
            in_specs=[pl.BlockSpec(memory_space=pl.ANY)] * 3,
            out_specs=(pl.BlockSpec(memory_space=pltpu.VMEM),) * 2,
            scratch_shapes=[
                vmem(data_tile.shape, jnp.bfloat16),
                vmem(w_factor.shape, jnp.float32),
                vmem(h_factor.shape, jnp.float32),
                vmem((SUB, wide), jnp.float32),
                vmem((cols, SUB, wide), jnp.float32),
                vmem((ITERS, rows, rank, hp), jnp.bfloat16),
                vmem((ITERS, rows, rank + 1, hp), jnp.float32),
                vmem((ITERS, rows, rank + 1, hp), jnp.float32),
                vmem((cols, SUB + 1, wide), jnp.float32),
                vmem((cols, SUB + 1, wide), jnp.float32),
                vmem((ITERS, rank + 1, half), jnp.float32),
                vmem((ITERS, rank + 1, half), jnp.float32),
                vmem((ITERS, cols // 2, rank + 1, half), jnp.float32),
                vmem((ITERS, rank, half), jnp.float32),
                vmem((ITERS, rank, half), jnp.float32),
                dma((3,)),
                dma((cols,)),
                dma((cols,)),
                dma((ITERS, rows)),
                dma((ITERS, rows)),
                dma((ITERS, rows)),
                dma((ITERS, rows)),
                dma((cols,)),
                dma((cols,)),
                dma((ITERS,)),
                dma((ITERS,)),
                dma((ITERS, cols // 2)),
                dma((ITERS, cols // 2)),
                dma((ITERS,)),
                dma((ITERS,)),
            ],
            compiler_params=pltpu.CompilerParams(collective_id=0, has_side_effects=True),
        )(data_tile, w_factor, h_factor)
        return pl.pallas_call(
            finish,
            out_shape=(
                jax.ShapeDtypeStruct(w_factor.shape, jnp.float32),
                jax.ShapeDtypeStruct(h_factor.shape, jnp.float32),
            ),
            in_specs=[pl.BlockSpec(memory_space=pltpu.VMEM)] * 2,
            out_specs=(pl.BlockSpec(memory_space=pl.ANY),) * 2,
            scratch_shapes=[dma((2,))],
            compiler_params=pltpu.CompilerParams(vmem_limit_bytes=2**20),
        )(w_new, h_new)

    placed = (P("rows", "cols"), P(None, ("rows", "cols")), P(None, ("cols", "rows")))
    return jax.shard_map(
        shards,
        mesh=mesh,
        in_specs=placed,
        out_specs=(P(None, ("rows", "cols")), P(None, ("cols", "rows"))),
        check_vma=False,
    )
```

```python
import functools

import jax
import jax.numpy as jnp
from jax import lax
from jax.experimental import pallas as pl
from jax.experimental.pallas import tpu as pltpu
from jax.sharding import PartitionSpec as P

ITERS = 2

damping = 0.75

MESH = pl.DeviceIdType.MESH
SUB = 8
LANES = 128


def partner(me, d, n):
    if n & (n - 1) == 0:
        out, bit = me, 1
        while bit < n:
            if d & bit:
                out = out + bit * (1 - 2 * (lax.rem(lax.div(me, bit), 2)))
            bit *= 2
        return out
    return lax.rem(d + n - me, n)


def fold(block):
    return jnp.concatenate([block[s : s + SUB] for s in range(0, block.shape[0], SUB)], axis=1)


def unfold(dense, groups, width):
    return jnp.concatenate([dense[:, s * width : (s + 1) * width] for s in range(groups)], axis=0)


def chunk_order(it, rows):
    return [*range(rows - 1, 0, -1), 0]


def as_column(row, rank):
    spread = jnp.broadcast_to(row[:, 0:rank], (rank, rank))
    at = lax.broadcasted_iota(jnp.int32, (rank, rank), 0) == lax.broadcasted_iota(jnp.int32, (rank, rank), 1)
    return jnp.sum(jnp.where(at, spread, 0.0), axis=1, keepdims=True)


def kernel(
    rows, cols, data_hbm, w_hbm, h_hbm, w_out, h_out,
    data_v, w_in, h_own, w_own, w_slots, h_slots, h_send, h_recv, w_send, w_recv,
    pair_send, pair_recv, chip_sums, half_send, half_recv,
    local_sem, wg_s, wg_r, hg_s, hg_r, hr_s, hr_r, wr_s, wr_r, ps_s, ps_r, cs_s, cs_r, hf_s, hf_r,
):
    c, r = lax.axis_index("cols"), lax.axis_index("rows")
    rank, wp = w_hbm.shape
    hp = h_hbm.shape[1]
    tr, tc = data_v.shape
    groups = rank // SUB
    used = groups * wp
    half = tr // 2
    chips = cols // 2
    chip, core = lax.div(c, 2), lax.rem(c, 2)

    load_w = pltpu.make_async_copy(w_hbm, w_in, local_sem.at[0])
    load_h = pltpu.make_async_copy(h_hbm, h_own, local_sem.at[1])
    load_data = pltpu.make_async_copy(data_hbm, data_v, local_sem.at[2])

    c_peers = [(d, partner(c, d, cols)) for d in range(1, cols)]
    r_peers = [(d, partner(r, d, rows)) for d in range(1, rows)]
    chip_peers = [(d, 2 * partner(chip, d, chips) + core) for d in range(1, chips)]
    barrier = pltpu.get_barrier_semaphore()
    for d, p in reversed(c_peers):
        pl.semaphore_signal(barrier, inc=1, device_id={"cols": p}, device_id_type=MESH)
    for d, p in reversed(r_peers):
        pl.semaphore_signal(barrier, inc=1, device_id={"rows": p}, device_id_type=MESH)

    load_w.start()
    load_h.start()
    load_data.start()
    load_w.wait()
    load_h.wait()
    w_own[:, 0:used] = fold(w_in[...])
    h_slots[0, 0] = h_own[...].astype(jnp.bfloat16)
    pl.semaphore_wait(barrier, cols - 1 + rows - 1)

    pending = []

    def send(src, dst, s_sem, r_sem, where):
        copy = pltpu.make_async_remote_copy(
            src_ref=src, dst_ref=dst, send_sem=s_sem, recv_sem=r_sem, device_id=where, device_id_type=MESH
        )
        copy.start()
        pending.append(copy)
        return copy

    def gather_h(it):
        return {
            d: send(h_slots.at[it, 0], h_slots.at[it, d], hg_s.at[it, d], hg_r.at[it, d], {"rows": p})
            for d, p in reversed(r_peers)
        }

    w_copies = [
        send(w_own, w_slots.at[c], wg_s.at[d], wg_r.at[d], {"cols": p}) for d, p in reversed(c_peers)
    ]
    h_copies = gather_h(0)
    h_now = h_own[...]
    w_slots[c] = w_own[...]
    load_data.wait()
    for copy in w_copies:
        copy.wait_recv()
    w_f32 = jnp.concatenate(
        [
            jnp.concatenate([w_slots[p, :, s * wp : (s + 1) * wp] for p in range(cols)], axis=1)
            for s in range(groups)
        ],
        axis=0,
    )

    for it in range(ITERS):
        last = it + 1 == ITERS
        w_block = w_f32.astype(jnp.bfloat16)
        w_rows = w_f32.T.astype(jnp.bfloat16)
        w_sum = jnp.sum(w_rows.astype(jnp.float32), axis=0, keepdims=True)
        w_part = jnp.zeros((rank, tr), jnp.float32)
        h_sum = jnp.zeros((SUB, rank), jnp.float32)
        h_sends = []
        for d in range(1, rows):
            h_copies[d].wait_recv()
        kept_chunks = []
        for d in chunk_order(it, rows):
            p = r if d == 0 else r_peers[d - 1][1]
            h_piece = h_slots[it, d]
            approx = jnp.dot(w_rows, h_piece, preferred_element_type=jnp.float32)
            if hp % LANES == 0:
                data = data_v[:, pl.ds(pl.multiple_of(p * hp, hp), hp)]
            else:
                per = LANES // hp
                base = pl.multiple_of(lax.div(p, per) * LANES, LANES)
                wide = data_v[:, pl.ds(base, LANES)].astype(jnp.float32)
                data = wide[:, 0:hp]
                for k in range(1, per):
                    data = jnp.where(lax.rem(p, per) == k, wide[:, k * hp : (k + 1) * hp], data)
            quotient = (data.astype(jnp.float32) / approx).astype(jnp.bfloat16)
            kept_chunks.append((d, p, h_piece, quotient))
        for d, p, h_piece, quotient in kept_chunks:
            h_part = jnp.dot(w_block, quotient, preferred_element_type=jnp.float32)
            h_send[it, d, 0:rank] = h_part
            h_send[it, d, rank : rank + 1, 0:rank] = w_sum
            if d > 0:
                h_sends.append(
                    send(h_send.at[it, d], h_recv.at[it, d], hr_s.at[it, d], hr_r.at[it, d], {"rows": p})
                )

        for d, p, h_piece, quotient in kept_chunks:
            w_part += lax.dot_general(
                h_piece, quotient, (((1,), (1,)), ((), ())), preferred_element_type=jnp.float32
            )
            h_sum += lax.dot_general(
                jnp.ones((SUB, hp), jnp.bfloat16), h_piece, (((1,), (1,)), ((), ())),
                preferred_element_type=jnp.float32,
            )

        if last:
            for p in range(cols):
                w_send[p, 0:SUB, 0:used] = fold(w_part[:, p * wp : (p + 1) * wp])
                w_send[p, SUB : SUB + 1, 0:rank] = h_sum[0:1]
            w_sends = [
                send(w_send.at[p], w_recv.at[d], wr_s.at[d], wr_r.at[d], {"cols": p})
                for d, p in reversed(c_peers)
            ]
        else:
            low, high = w_part[:, 0:half], w_part[:, half:tr]
            pair_send[it, 0:rank] = jnp.where(core == 0, high, low)
            pair_send[it, rank : rank + 1, 0:rank] = h_sum[0:1]
            pair = send(
                pair_send.at[it], pair_recv.at[it], ps_s.at[it], ps_r.at[it], {"cols": c + 1 - 2 * core}
            )
            kept = jnp.where(core == 0, low, high)
            pair.wait_recv()
            chip_sums[it, chip, 0:rank] = kept + pair_recv[it, 0:rank]
            chip_sums[it, chip, rank : rank + 1, 0:rank] = h_sum[0:1] + pair_recv[it, rank : rank + 1, 0:rank]
            chip_sends = [
                send(
                    chip_sums.at[it, chip], chip_sums.at[it, chip], cs_s.at[it, d], cs_r.at[it, d], {"cols": p}
                )
                for d, p in reversed(chip_peers)
            ]

        for copy in h_sends:
            copy.wait_recv()
        numer, total = h_send[it, 0, 0:rank], h_send[it, 0, rank : rank + 1, 0:rank]
        for d, p in r_peers:
            numer += h_recv[it, d, 0:rank]
            total += h_recv[it, d, rank : rank + 1, 0:rank]
        h_now = h_now * (1.0 - damping + damping * numer / as_column(total, rank))
        if last:
            h_out[...] = h_now
        else:
            h_slots[it + 1, 0] = h_now.astype(jnp.bfloat16)
            h_copies = gather_h(it + 1)

        if last:
            w_now = w_f32[:, 0:wp]
            for p in range(1, cols):
                w_now = jnp.where(c == p, w_f32[:, p * wp : (p + 1) * wp], w_now)
            numer, total = w_send[c, 0:SUB, 0:used], w_send[c, SUB : SUB + 1, 0:rank]
            for (d, p), copy in zip(c_peers, reversed(w_sends)):
                copy.wait_recv()
                numer += w_recv[d, 0:SUB, 0:used]
                total += w_recv[d, SUB : SUB + 1, 0:rank]
            numer = unfold(numer, groups, wp)
            w_out[...] = w_now * (1.0 - damping + damping * numer / as_column(total, rank))
        else:
            w_half = jnp.where(core == 0, w_f32[:, 0:half], w_f32[:, half:tr])
            for copy in chip_sends:
                copy.wait_recv()
            numer, total = chip_sums[it, 0, 0:rank], chip_sums[it, 0, rank : rank + 1, 0:rank]
            for p in range(1, chips):
                numer += chip_sums[it, p, 0:rank]
                total += chip_sums[it, p, rank : rank + 1, 0:rank]
            w_half = w_half * (1.0 - damping + damping * numer / as_column(total, rank))
            half_send[it] = w_half
            swap = send(
                half_send.at[it], half_recv.at[it], hf_s.at[it], hf_r.at[it], {"cols": c + 1 - 2 * core}
            )
            swap.wait_recv()
            theirs = half_recv[it]
            w_f32 = jnp.concatenate(
                [jnp.where(core == 0, w_half, theirs), jnp.where(core == 0, theirs, w_half)], axis=1
            )

    for copy in pending:
        copy.wait_send()


def finish(w_ref, h_ref, w_out, h_out, sems):
    copies = [
        pltpu.make_async_copy(w_ref, w_out, sems.at[0]),
        pltpu.make_async_copy(h_ref, h_out, sems.at[1]),
    ]
    for copy in copies:
        copy.start()
    for copy in copies:
        copy.wait()


def solution(mesh):
    rows, cols = mesh.shape["rows"], mesh.shape["cols"]

    def shards(data_tile, w_factor, h_factor):
        rank, wp = w_factor.shape
        hp = h_factor.shape[1]
        half = data_tile.shape[0] // 2
        wide = pl.cdiv(rank // SUB * wp, LANES) * LANES
        vmem, dma = pltpu.VMEM, pltpu.SemaphoreType.DMA
        w_new, h_new = pl.pallas_call(
            functools.partial(kernel, rows, cols),
            out_shape=(
                pltpu.VMEM(w_factor.shape, jnp.float32),
                pltpu.VMEM(h_factor.shape, jnp.float32),
            ),
            in_specs=[pl.BlockSpec(memory_space=pl.ANY)] * 3,
            out_specs=(pl.BlockSpec(memory_space=pltpu.VMEM),) * 2,
            scratch_shapes=[
                vmem(data_tile.shape, jnp.bfloat16),
                vmem(w_factor.shape, jnp.float32),
                vmem(h_factor.shape, jnp.float32),
                vmem((SUB, wide), jnp.float32),
                vmem((cols, SUB, wide), jnp.float32),
                vmem((ITERS, rows, rank, hp), jnp.bfloat16),
                vmem((ITERS, rows, rank + 1, hp), jnp.float32),
                vmem((ITERS, rows, rank + 1, hp), jnp.float32),
                vmem((cols, SUB + 1, wide), jnp.float32),
                vmem((cols, SUB + 1, wide), jnp.float32),
                vmem((ITERS, rank + 1, half), jnp.float32),
                vmem((ITERS, rank + 1, half), jnp.float32),
                vmem((ITERS, cols // 2, rank + 1, half), jnp.float32),
                vmem((ITERS, rank, half), jnp.float32),
                vmem((ITERS, rank, half), jnp.float32),
                dma((3,)),
                dma((cols,)),
                dma((cols,)),
                dma((ITERS, rows)),
                dma((ITERS, rows)),
                dma((ITERS, rows)),
                dma((ITERS, rows)),
                dma((cols,)),
                dma((cols,)),
                dma((ITERS,)),
                dma((ITERS,)),
                dma((ITERS, cols // 2)),
                dma((ITERS, cols // 2)),
                dma((ITERS,)),
                dma((ITERS,)),
            ],
            compiler_params=pltpu.CompilerParams(collective_id=0, has_side_effects=True),
        )(data_tile, w_factor, h_factor)
        return pl.pallas_call(
            finish,
            out_shape=(
                jax.ShapeDtypeStruct(w_factor.shape, jnp.float32),
                jax.ShapeDtypeStruct(h_factor.shape, jnp.float32),
            ),
            in_specs=[pl.BlockSpec(memory_space=pltpu.VMEM)] * 2,
            out_specs=(pl.BlockSpec(memory_space=pl.ANY),) * 2,
            scratch_shapes=[dma((2,))],
            compiler_params=pltpu.CompilerParams(vmem_limit_bytes=2**20),
        )(w_new, h_new)

    placed = (P("rows", "cols"), P(None, ("rows", "cols")), P(None, ("cols", "rows")))
    return jax.shard_map(
        shards,
        mesh=mesh,
        in_specs=placed,
        out_specs=(P(None, ("rows", "cols")), P(None, ("cols", "rows"))),
        check_vma=False,
    )
```
